1024 devices in a mesh: seq: 16 (over x, core), chan: 64 (over y, z).
Axes of the slice: x: 8, y: 8, z: 8, core: 2. Of those that a mesh axis runs over, the one named last changes fastest.
Arguments:
- tokens: bfloat16 [2048, 8192], P('seq', 'chan'), may hold values from -6 to 6
- in_weight: bfloat16 [8192, 3, 8192], P(None, None, 'chan'), may hold values from -0.0625 to 0.0625
- long_filter: float32 [2048, 8192], P('seq', 'chan'), may hold values from -1 to 1
- grad_out: bfloat16 [2048, 8192], P('seq', 'chan'), may hold values from -6 to 6
Outputs:
- gated_out: bfloat16 [2048, 8192], P('seq', 'chan')
- grad_proj: bfloat16 [2048, 3, 8192], P('seq', None, 'chan')
- grad_filter: float32 [2048, 8192], P('seq', 'chan')
The draws below stay inside these ranges and needn't reach their ends.
All inputs are finite; a program needn't handle non-finite values.
Results may differ from the reference program's by a relative error of at most 0.0064.
Values may be sent and summed in bfloat16 or wider, within the bound.
A program may use at most 64 MiB of HBM per device.

```python
import jax
import jax.numpy as jnp

D = 8192
SEQ = 2048


def draw_long_filter(key, part):
    noise_key, rate_key = jax.random.split(key)
    filter_taps = jax.random.truncated_normal(noise_key, -4.0, 4.0, (SEQ, D), jnp.float32)
    low_log = jnp.log(30.0)
    high_log = jnp.log(4.0 * SEQ)
    decay_span = jnp.exp(jax.random.uniform(rate_key, (1, D), jnp.float32, low_log, high_log))
    steps_pos = jnp.arange(SEQ, dtype=jnp.float32)[:, None]
    return filter_taps * jnp.exp(-steps_pos / decay_span) / jnp.sqrt(jnp.minimum(decay_span, 1.0 * SEQ))


def block_levels(key, dims, pieces, smallest, high):
    loudness = 1.0
    for position, shards_of in pieces:
        heights = jax.random.uniform(jax.random.fold_in(jax.random.fold_in(key, 6), position), (shards_of,), jnp.float32, smallest / len(pieces), high / len(pieces))
        loudness = loudness * jnp.repeat(jnp.exp(heights), dims[position] // shards_of).reshape((-1,) + (1,) * (len(dims) - 1 - position))
    return loudness


def centred(own_key, dims, scale, most, pieces=(), held_as=jnp.bfloat16):
    result = scale * jax.random.normal(own_key, dims, jnp.float32)
    if pieces:
        result = result * block_levels(own_key, dims, pieces, -0.22, 0.18)
    return jnp.clip(result, -most, most).astype(held_as)


def setup_inputs(seed: int = 0) -> dict:
    key_list = jax.random.split(jax.random.key(seed), 5)
    return {
        "tokens": centred(key_list[0], (SEQ, D), 1.0, 6.0, ((0, 16), (1, 64))),
        "in_weight": centred(key_list[1], (D, 3, D), D ** -0.5, 0.0625, ((2, 64),)),
        "long_filter": draw_long_filter(jax.random.fold_in(key_list[4], 71), 0),
        "grad_out": centred(key_list[3], (SEQ, D), 1.0, 6.0, ((0, 16), (1, 64))),
    }


def reference(tokens, in_weight, long_filter, grad_out):
    projection = jnp.dot(tokens, in_weight.reshape(D, 3 * D), preferred_element_type=jnp.float32)
    projection = projection.astype(jnp.bfloat16).reshape(SEQ, 3, D)
    gate_in = projection[:, 0, :].astype(jnp.float32)
    gate_out = projection[:, 1, :].astype(jnp.float32)
    values = projection[:, 2, :].astype(jnp.float32)
    grad_dense = grad_out.astype(jnp.float32)
    source = gate_in * values
    grad_conv = grad_dense * gate_out
    padded = 2 * SEQ
    spec_source = jnp.fft.rfft(source, n=padded, axis=0)
    spec_filter = jnp.fft.rfft(long_filter, n=padded, axis=0)
    spec_grad = jnp.fft.rfft(grad_conv, n=padded, axis=0)
    conv_out = jnp.fft.irfft(spec_source * spec_filter, n=padded, axis=0)[:SEQ]
    grad_source = jnp.fft.irfft(jnp.conj(spec_filter) * spec_grad, n=padded, axis=0)[:SEQ]
    grad_filter = jnp.fft.irfft(jnp.conj(spec_source) * spec_grad, n=padded, axis=0)[:SEQ]
    gated_out = (gate_out * conv_out).astype(jnp.bfloat16)
    grad_proj = jnp.stack([grad_source * values, grad_dense * conv_out, grad_source * gate_in], axis=1)
    return gated_out, grad_proj.astype(jnp.bfloat16), grad_filter.astype(jnp.float32)
```

```python
import functools
import math

import jax
import jax.numpy as jnp
import ml_dtypes
import numpy as np
from jax import lax
from jax.experimental import pallas as pl
from jax.experimental.pallas import tpu as pltpu
from jax.sharding import PartitionSpec as P

MESH = pl.DeviceIdType.MESH
SUBS = 2


def grid_of(chans):
    columns = 1
    while columns * columns < chans:
        columns *= 2
    return chans // columns, columns


def split_table(table):
    high = table.astype(ml_dtypes.bfloat16)
    low = (table - high.astype(np.float64)).astype(ml_dtypes.bfloat16)
    return high, low


def tables(rows):
    angle = math.pi * np.outer(np.arange(2 * rows), 2 * np.arange(rows) + 1) / (2 * rows)
    forward = np.concatenate([np.cos(angle), -np.sin(angle)], axis=1)[:rows]
    inverse = np.concatenate([np.cos(angle), -np.sin(angle)], axis=1).T / rows
    return np.concatenate(split_table(forward), axis=0), np.stack(split_table(inverse))


def dot(left, right):
    return jnp.dot(left, right, preferred_element_type=jnp.float32)


def split(value):
    high = value.astype(jnp.bfloat16)
    return high, (value - high.astype(jnp.float32)).astype(jnp.bfloat16)


def body(
    ny, nz, nseq,
    tok_hbm, w_hbm, filt_hbm, gout_hbm, fwd_hbm, inv_hbm,
    gated, gproj, gfilt,
    tok, filt, gout, w, fwd, inv, abuf, bbuf, acc,
    fsend, frecv, fspec, xsend, xrecv, xspec, prod, ysend, yrecv,
    local_sem, p1_send, p1_recv, ring_send, ring_recv, f_send, f_recv, x_send, x_recv, y_send, y_recv,
):
    rows, width = filt.shape
    half = rows // 2
    per = width // nseq
    seq = lax.axis_index("seq")
    chan = lax.axis_index("chan")
    y, z = chan // nz, chan % nz

    weights = [
        pltpu.make_async_copy(w_hbm.at[b], w.at[:, pl.ds(b * width, width)], local_sem.at[b])
        for b in range(3)
    ]
    constants = [
        pltpu.make_async_copy(fwd_hbm, fwd, local_sem.at[3]),
        pltpu.make_async_copy(inv_hbm, inv, local_sem.at[4]),
    ]
    inputs = [
        pltpu.make_async_copy(tok_hbm, tok, local_sem.at[5]),
        pltpu.make_async_copy(filt_hbm, filt, local_sem.at[6]),
        pltpu.make_async_copy(gout_hbm, gout, local_sem.at[7]),
    ]
    for copy in inputs + constants + weights:
        copy.start()

    barrier = pltpu.get_barrier_semaphore()

    def seq_peer(step):
        return (lax.rem(seq + step, nseq), chan)

    def z_peer(step):
        return (seq, y * nz + lax.rem(z + step, nz))

    def y_peer(step):
        return (seq, lax.rem(y + step, ny) * nz + z)

    for peer, count in ((z_peer, nz), (y_peer, ny), (seq_peer, nseq)):
        def greet(step, carry, peer=peer):
            pl.semaphore_signal(barrier, inc=1, device_id=peer(step), device_id_type=MESH)
            return carry
        lax.fori_loop(1, count, greet, 0)

    for copy in inputs:
        copy.wait()
    abuf[y, z] = tok[:half]
    bbuf[z, y] = tok[half:]
    fsend[...] = filt[...].T.reshape(nseq, per, rows)
    pl.semaphore_wait(barrier, nz + ny + nseq - 3)

    def first(which, step):
        source = tok.at[pl.ds(which * half, half)]
        target = abuf.at[y, z] if which == 0 else bbuf.at[z, y]
        return pltpu.make_async_remote_copy(
            source, target, p1_send.at[which, step], p1_recv.at[which, step],
            device_id=(z_peer if which == 0 else y_peer)(step), device_id_type=MESH,
        )

    def each(count, action):
        def step_of(step, carry):
            action(step)
            return carry
        lax.fori_loop(1, count, step_of, 0)

    each(nz, lambda step: first(0, step).start())
    each(ny, lambda step: first(1, step).start())

    def exchange(source, target, send, recv, step):
        to = lax.rem(seq + step, nseq)
        return pltpu.make_async_remote_copy(
            source.at[to], target.at[seq], send.at[step], recv.at[step],
            device_id=(to, chan), device_id_type=MESH,
        )

    filters = functools.partial(exchange, fsend, frecv, f_send, f_recv)
    each(nseq, lambda step: filters(step).start())
    frecv[seq] = fsend[seq]

    def ring(direction, step, piece, arriving=False):
        sign = 1 if direction % 2 == 0 else -1
        buffer, place, count, across = (abuf, y, ny, nz) if direction < 2 else (bbuf, z, nz, ny)
        hop = (count + sign) % count
        chunk = lax.rem(place + count - sign * (step - (0 if arriving else 1)), count)
        block = buffer.at[chunk, pl.ds(piece * (across // SUBS), across // SUBS)]
        return pltpu.make_async_remote_copy(
            block, block, ring_send.at[direction, step, piece], ring_recv.at[direction, step, piece],
            device_id=(y_peer if direction < 2 else z_peer)(hop), device_id_type=MESH,
        ), chunk

    def multiply(direction, chunk, piece):
        if direction < 2:
            count = nz // SUBS
            left = jnp.concatenate([abuf[chunk, piece * count + i] for i in range(count)], axis=1)
            right = w[pl.ds(pl.multiple_of((chunk * nz + piece * count) * width, width), count * width)]
            acc[:half] += dot(left, right)
        else:
            count = ny // SUBS
            left = jnp.concatenate([bbuf[chunk, piece * count + i] for i in range(count)], axis=1)
            right = jnp.concatenate(
                [
                    w[pl.ds(pl.multiple_of(((piece * count + i) * nz + chunk) * width, width), width)]
                    for i in range(count)
                ],
                axis=0,
            )
            acc[half:] += dot(left, right)

    def sends(direction, step, piece):
        last = (ny if direction < 2 else nz) // 2
        if step < last:
            return True
        return step == last and (piece < SUBS // 2) == (direction % 2 == 0)

    each(nz, lambda step: first(0, step).wait_recv())
    each(ny, lambda step: first(1, step).wait_recv())
    for piece in range(SUBS):
        for direction in range(4):
            if sends(direction, 1, piece):
                ring(direction, 1, piece)[0].start()

    for copy in weights:
        copy.wait()
    acc[...] = jnp.zeros_like(acc)
    for piece in range(SUBS):
        multiply(0, y, piece)
        multiply(2, z, piece)

    each(nseq, lambda step: filters(step).wait_recv())
    for copy in constants:
        copy.wait()
    high, low = split(frecv[...].reshape(nseq * per, rows))
    fspec[...] = (
        dot(jnp.concatenate([high, high], axis=1), fwd[...]) + dot(low, fwd[:rows])
    ).reshape(nseq, per, 2 * rows)

    for step in range(1, max(ny, nz) // 2 + 1):
        for piece in range(SUBS):
            arrived = []
            for direction in range(4):
                if sends(direction, step, piece):
                    copy, chunk = ring(direction, step, piece, arriving=True)
                    copy.wait_recv()
                    if sends(direction, step + 1, piece):
                        ring(direction, step + 1, piece)[0].start()
                    arrived.append((direction, chunk))
            for direction, chunk in arrived:
                multiply(direction, chunk, piece)

    projection = acc[...].astype(jnp.bfloat16).astype(jnp.float32)
    gate_in, gate_out, values = (projection[:, b * width : (b + 1) * width] for b in range(3))
    grad_dense = gout[...].astype(jnp.float32)
    source = (gate_in * values).T.reshape(nseq, per, rows)
    grad_conv = (grad_dense * gate_out).T.reshape(nseq, per, rows)
    xsend[...] = jnp.concatenate([source, grad_conv], axis=1).astype(jnp.bfloat16)
    signals = functools.partial(exchange, xsend, xrecv, x_send, x_recv)
    each(nseq, lambda step: signals(step).start())
    xrecv[seq] = xsend[seq]
    each(nseq, lambda step: signals(step).wait_recv())

    received = xrecv[...].reshape(nseq * 2 * per, rows)
    xspec[...] = dot(jnp.concatenate([received, received], axis=1), fwd[...]).reshape(
        nseq, 2 * per, 2 * rows
    )

    def spectrum(ref, block, first_row):
        return (
            ref[block, first_row : first_row + per, :rows],
            ref[block, first_row : first_row + per, rows:],
        )

    for out in range(nseq):
        re, im = 0.0, 0.0
        for j in range(out + 1):
            f_re, f_im = spectrum(fspec, j, 0)
            s_re, s_im = spectrum(xspec, out - j, 0)
            re = re + (f_re * s_re - f_im * s_im)
            im = im + (f_re * s_im + f_im * s_re)
        prod[out, :per, :rows] = re
        prod[out, :per, rows:] = im
        re, im, re2, im2 = 0.0, 0.0, 0.0, 0.0
        for j in range(nseq - out):
            g_re, g_im = spectrum(xspec, out + j, per)
            f_re, f_im = spectrum(fspec, j, 0)
            s_re, s_im = spectrum(xspec, j, 0)
            re = re + (f_re * g_re + f_im * g_im)
            im = im + (f_re * g_im - f_im * g_re)
            re2 = re2 + (s_re * g_re + s_im * g_im)
            im2 = im2 + (s_re * g_im - s_im * g_re)
        prod[out, per : 2 * per, :rows] = re
        prod[out, per : 2 * per, rows:] = im
        prod[out, 2 * per :, :rows] = re2
        prod[out, 2 * per :, rows:] = im2

    high, low = split(prod[...].reshape(nseq * 3 * per, 2 * rows))
    prod[...] = (dot(high, inv[0]) + dot(low, inv[0]) + dot(high, inv[1])).reshape(
        nseq, 3 * per, 2 * rows
    )
    for block in range(nseq):
        conv = prod[block, :per, :rows]
        grads = prod[block, per:, :rows]
        if block > 0:
            conv = conv + prod[block - 1, :per, rows:]
        if block < nseq - 1:
            grads = grads - prod[block + 1, per:, rows:]
        of_filter = grads[per:]
        rest = of_filter - of_filter.astype(jnp.bfloat16).astype(jnp.float32)
        ysend[block] = jnp.concatenate([conv, grads, rest], axis=0).astype(jnp.bfloat16)
    results = functools.partial(exchange, ysend, yrecv, y_send, y_recv)
    each(nseq, lambda step: results(step).start())
    yrecv[seq] = ysend[seq]
    each(nseq, lambda step: results(step).wait_recv())

    back = yrecv[...].astype(jnp.float32)
    conv_out = back[:, :per].reshape(width, rows).T
    grad_source = back[:, per : 2 * per].reshape(width, rows).T
    of_filter = (back[:, 2 * per : 3 * per] + back[:, 3 * per :]).reshape(width, rows).T
    gated[...] = (gate_out * conv_out).astype(jnp.bfloat16)
    gproj[0] = (grad_source * values).astype(jnp.bfloat16)
    gproj[1] = (grad_dense * conv_out).astype(jnp.bfloat16)
    gproj[2] = (grad_source * gate_in).astype(jnp.bfloat16)
    gfilt[...] = of_filter

    each(nz, lambda step: first(0, step).wait_send())
    each(ny, lambda step: first(1, step).wait_send())
    for step in range(1, max(ny, nz) // 2 + 1):
        for piece in range(SUBS):
            for direction in range(4):
                if sends(direction, step, piece):
                    ring(direction, step, piece)[0].wait_send()
    each(nseq, lambda step: filters(step).wait_send())
    each(nseq, lambda step: signals(step).wait_send())
    each(nseq, lambda step: results(step).wait_send())


def per_device(tokens, in_weight, long_filter, grad_out):
    rows, width = long_filter.shape
    depth = in_weight.shape[0]
    nseq = lax.axis_size("seq")
    ny, nz = grid_of(lax.axis_size("chan"))
    per = width // nseq
    forward, inverse = tables(rows)
    vmem = pl.BlockSpec(memory_space=pltpu.VMEM)
    hbm = pl.BlockSpec(memory_space=pltpu.HBM)
    bf16, f32 = jnp.bfloat16, jnp.float32
    dma = pltpu.SemaphoreType.DMA
    steps = max(ny, nz) // 2 + 1
    gated_out, grad_proj, grad_filter = pl.pallas_call(
        functools.partial(body, ny, nz, nseq),
        name="gather_project_convolve",
        out_shape=(
            jax.ShapeDtypeStruct((rows, width), bf16),
            jax.ShapeDtypeStruct((3, rows, width), bf16),
            jax.ShapeDtypeStruct((rows, width), f32),
        ),
        in_specs=[hbm] * 6,
        out_specs=(vmem, vmem, vmem),
        scratch_shapes=[
            pltpu.VMEM((rows, width), bf16),
            pltpu.VMEM((rows, width), f32),
            pltpu.VMEM((rows, width), bf16),
            pltpu.VMEM((depth, 3 * width), bf16),
            pltpu.VMEM(forward.shape, bf16),
            pltpu.VMEM(inverse.shape, bf16),
            pltpu.VMEM((ny, nz, rows // 2, width), bf16),
            pltpu.VMEM((nz, ny, rows // 2, width), bf16),
            pltpu.VMEM((rows, 3 * width), f32),
            pltpu.VMEM((nseq, per, rows), f32),
            pltpu.VMEM((nseq, per, rows), f32),
            pltpu.VMEM((nseq, per, 2 * rows), f32),
            pltpu.VMEM((nseq, 2 * per, rows), bf16),
            pltpu.VMEM((nseq, 2 * per, rows), bf16),
            pltpu.VMEM((nseq, 2 * per, 2 * rows), f32),
            pltpu.VMEM((nseq, 3 * per, 2 * rows), f32),
            pltpu.VMEM((nseq, 4 * per, rows), bf16),
            pltpu.VMEM((nseq, 4 * per, rows), bf16),
            dma((8,)),
            dma((2, max(ny, nz))),
            dma((2, max(ny, nz))),
            dma((4, steps, SUBS)),
            dma((4, steps, SUBS)),
            dma((nseq,)),
            dma((nseq,)),
            dma((nseq,)),
            dma((nseq,)),
            dma((nseq,)),
            dma((nseq,)),
        ],
        compiler_params=pltpu.CompilerParams(
            collective_id=0, has_side_effects=True, vmem_limit_bytes=56 * 2**20
        ),
    )(
        tokens,
        jnp.transpose(in_weight, (1, 0, 2)),
        long_filter,
        grad_out,
        jnp.asarray(forward),
        jnp.asarray(inverse),
    )
    return gated_out, jnp.transpose(grad_proj, (1, 0, 2)), grad_filter


def solution(mesh):
    in_specs = (P("seq", "chan"), P(None, None, "chan"), P("seq", "chan"), P("seq", "chan"))
    out_specs = (P("seq", "chan"), P("seq", None, "chan"), P("seq", "chan"))
    return jax.shard_map(
        per_device, mesh=mesh, in_specs=in_specs, out_specs=out_specs, check_vma=False
    )
```

```python
import functools
import math

import jax
import jax.numpy as jnp
import ml_dtypes
import numpy as np
from jax import lax
from jax.experimental import pallas as pl
from jax.experimental.pallas import tpu as pltpu
from jax.sharding import PartitionSpec as P

MESH = pl.DeviceIdType.MESH


def grid_of(chans):
    columns = 1
    while columns * columns < chans:
        columns *= 2
    return chans // columns, columns


def split_table(table):
    high = table.astype(ml_dtypes.bfloat16)
    low = (table - high.astype(np.float64)).astype(ml_dtypes.bfloat16)
    return high, low


def tables(rows):
    angle = math.pi * np.outer(np.arange(2 * rows), 2 * np.arange(rows) + 1) / (2 * rows)
    forward = np.concatenate([np.cos(angle), -np.sin(angle)], axis=1)[:rows]
    inverse = np.concatenate([np.cos(angle), -np.sin(angle)], axis=1).T / rows
    return np.concatenate(split_table(forward), axis=0), np.stack(split_table(inverse))


def dot(left, right):
    return jnp.dot(left, right, preferred_element_type=jnp.float32)


def split(value):
    high = value.astype(jnp.bfloat16)
    return high, (value - high.astype(jnp.float32)).astype(jnp.bfloat16)


def body(
    ny, nz, nseq,
    tok_hbm, w_hbm, filt_hbm, gout_hbm, fwd_hbm, inv_hbm,
    gated, gproj, gfilt,
    filt, gout, w, fwd, inv, tokens, acc,
    fsend, frecv, fspec, xsend, xrecv, xspec, prod, ysend, yrecv,
    local_sem, z_send, z_recv, ring_send, ring_recv, f_send, f_recv, x_send, x_recv, y_send, y_recv,
):
    rows, width = filt.shape
    half = rows // 2
    per = width // nseq
    seq = lax.axis_index("seq")
    chan = lax.axis_index("chan")
    y, z = chan // nz, chan % nz

    weights = [
        pltpu.make_async_copy(w_hbm.at[b], w.at[:, pl.ds(b * width, width)], local_sem.at[b])
        for b in range(3)
    ]
    constants = [
        pltpu.make_async_copy(fwd_hbm, fwd, local_sem.at[3]),
        pltpu.make_async_copy(inv_hbm, inv, local_sem.at[4]),
    ]
    inputs = [
        pltpu.make_async_copy(tok_hbm, tokens.at[z, y], local_sem.at[5]),
        pltpu.make_async_copy(filt_hbm, filt, local_sem.at[6]),
        pltpu.make_async_copy(gout_hbm, gout, local_sem.at[7]),
    ]
    for copy in inputs + constants + weights:
        copy.start()

    barrier = pltpu.get_barrier_semaphore()
    up, down = (seq, lax.rem(y + 1, ny) * nz + z), (seq, lax.rem(y + ny - 1, ny) * nz + z)

    def greet(peer):
        pl.semaphore_signal(barrier, inc=1, device_id=peer, device_id_type=MESH)

    def each(first, last, action):
        def step_of(step, carry):
            action(step)
            return carry
        lax.fori_loop(first, last, step_of, 0)

    greet(up)
    greet(down)
    each(z + 1, nz, lambda other: greet((seq, y * nz + other)))

    @pl.when(seq != 0)
    def _():
        each(1, nseq, lambda step: greet((lax.rem(seq + step, nseq), chan)))

    for copy in inputs:
        copy.wait()
    fsend[...] = filt[...].T.reshape(nseq, per, rows)
    frecv[seq] = fsend[seq]
    acc[...] = jnp.zeros_like(acc)
    pl.semaphore_wait(barrier, 2 + z + jnp.where(seq == 0, nseq - 1, nseq - 2))

    def along_z(other):
        return pltpu.make_async_remote_copy(
            tokens.at[z, y], tokens.at[z, y], z_send.at[other], z_recv.at[z],
            device_id=(seq, y * nz + other), device_id_type=MESH,
        )

    def from_z(other):
        return pltpu.make_async_remote_copy(
            tokens.at[other, y], tokens.at[other, y], z_send.at[other], z_recv.at[other],
            device_id=(seq, y * nz + other), device_id_type=MESH,
        )

    def column(place):
        if place == 0:
            return z
        later = jnp.where(place < z, place, place + 1)
        return jnp.where(z == 0, place, 0 if place == nz - 1 else later)

    columns = [column(place) for place in range(nz)]

    last = ny // 2
    rows_up = [lax.rem(y + ny - step, ny) for step in range(last + 1)]
    rows_down = [lax.rem(y + step, ny) for step in range(last + 1)]

    def ring(way, place, step, arriving=False):
        chunk = (rows_up, rows_down)[way][step if arriving else step - 1]
        block = tokens.at[columns[place], chunk]
        if step == last:
            block = block.at[pl.ds(way * half, half)]
        return pltpu.make_async_remote_copy(
            block, block, ring_send.at[way, place, step], ring_recv.at[way, place, step],
            device_id=(up, down)[way], device_id_type=MESH,
        )

    def multiply(place, chunks):
        left = [tokens[columns[place], chunk] for chunk in chunks]
        right = [
            w[pl.ds(pl.multiple_of((chunk * nz + columns[place]) * width, width), width)]
            for chunk in chunks
        ]
        acc[...] += dot(jnp.concatenate(left, axis=1), jnp.concatenate(right, axis=0))

    def exchange(source, target, send, recv, step):
        to = lax.rem(seq + step, nseq)
        return pltpu.make_async_remote_copy(
            source.at[to], target.at[seq], send.at[step], recv.at[step],
            device_id=(to, chan), device_id_type=MESH,
        )

    others = sorted(range(1, nseq), key=lambda step: abs(step - nseq // 2))
    filters = functools.partial(exchange, fsend, frecv, f_send, f_recv)
    signals = functools.partial(exchange, xsend, xrecv, x_send, x_recv)
    results = functools.partial(exchange, ysend, yrecv, y_send, y_recv)

    each(0, z, lambda other: along_z(other).start())

    def first_filters(step):
        @pl.when(lax.rem(seq + step, nseq) != 0)
        def _():
            filters(step).start()

    def other_filters(step):
        @pl.when(step != seq)
        def _():
            filters(step).wait_recv()

    events = sorted(
        ((place, step) for place in range(nz) for step in range(last + 1)),
        key=lambda event: (event[0] + event[1], event[0]),
    )
    for place, step in events:
        if step == 0 and place > 0:
            from_z(columns[place]).wait_recv()

            @pl.when(columns[place] > z)
            def _(place=place):
                along_z(columns[place]).start()

        if step > 0:
            ring(0, place, step, arriving=True).wait_recv()
            ring(1, place, step, arriving=True).wait_recv()
        if step < last:
            ring(0, place, step + 1).start()
            ring(1, place, step + 1).start()
        if (place, step) == (0, 0):
            each(1, nseq, first_filters)
            for copy in weights:
                copy.wait()
        if step in (0, last):
            multiply(place, [rows_up[step]])
        else:
            multiply(place, [rows_up[step], rows_down[step]])
        if (place, step) == (nz - 1, 0):
            @pl.when(seq != 0)
            def _():
                filters(seq).wait_recv()
                filters(nseq - seq).start()
        if (place, step) == (nz - 1, last - 1):
            each(1, nseq, other_filters)

            for copy in constants:
                copy.wait()
            high, low = split(frecv[...].reshape(nseq * per, rows))
            fspec[...] = (
                dot(jnp.concatenate([high, high], axis=1), fwd[...]) + dot(low, fwd[:rows])
            ).reshape(nseq, per, 2 * rows)

    projection = acc[...].astype(jnp.bfloat16).astype(jnp.float32)
    gate_in, gate_out, values = (projection[:, b * width : (b + 1) * width] for b in range(3))
    grad_dense = gout[...].astype(jnp.float32)
    source = (gate_in * values).T.reshape(nseq, per, rows)
    grad_conv = (grad_dense * gate_out).T.reshape(nseq, per, rows)
    xsend[...] = jnp.concatenate([source, grad_conv], axis=1).astype(jnp.bfloat16)
    for step in others:
        signals(step).start()
    xrecv[seq] = xsend[seq]
    for step in others:
        signals(step).wait_recv()

    received = xrecv[...].reshape(nseq * 2 * per, rows)
    xspec[...] = dot(jnp.concatenate([received, received], axis=1), fwd[...]).reshape(
        nseq, 2 * per, 2 * rows
    )

    def spectrum(ref, block, first_row):
        return (
            ref[block, first_row : first_row + per, :rows],
            ref[block, first_row : first_row + per, rows:],
        )

    for out in range(nseq):
        re, im = 0.0, 0.0
        for j in range(out + 1):
            f_re, f_im = spectrum(fspec, j, 0)
            s_re, s_im = spectrum(xspec, out - j, 0)
            re = re + (f_re * s_re - f_im * s_im)
            im = im + (f_re * s_im + f_im * s_re)
        prod[out, :per, :rows] = re
        prod[out, :per, rows:] = im
        re, im, re2, im2 = 0.0, 0.0, 0.0, 0.0
        for j in range(nseq - out):
            g_re, g_im = spectrum(xspec, out + j, per)
            f_re, f_im = spectrum(fspec, j, 0)
            s_re, s_im = spectrum(xspec, j, 0)
            re = re + (f_re * g_re + f_im * g_im)
            im = im + (f_re * g_im - f_im * g_re)
            re2 = re2 + (s_re * g_re + s_im * g_im)
            im2 = im2 + (s_re * g_im - s_im * g_re)
        prod[out, per : 2 * per, :rows] = re
        prod[out, per : 2 * per, rows:] = im
        prod[out, 2 * per :, :rows] = re2
        prod[out, 2 * per :, rows:] = im2

    high, low = split(prod[...].reshape(nseq * 3 * per, 2 * rows))
    prod[...] = (dot(high, inv[0]) + dot(low, inv[0]) + dot(high, inv[1])).reshape(
        nseq, 3 * per, 2 * rows
    )
    for block in range(nseq):
        conv = prod[block, :per, :rows]
        grads = prod[block, per:, :rows]
        if block > 0:
            conv = conv + prod[block - 1, :per, rows:]
        if block < nseq - 1:
            grads = grads - prod[block + 1, per:, rows:]
        ysend[block] = jnp.concatenate([conv, grads], axis=0).astype(jnp.bfloat16)
    for step in others:
        results(step).start()
    yrecv[seq] = ysend[seq]
    for step in others:
        results(step).wait_recv()

    back = yrecv[...].astype(jnp.float32)
    conv_out = back[:, :per].reshape(width, rows).T
    grad_source = back[:, per : 2 * per].reshape(width, rows).T
    of_filter = back[:, 2 * per :].reshape(width, rows).T
    gated[...] = (gate_out * conv_out).astype(jnp.bfloat16)
    gproj[0] = (grad_source * values).astype(jnp.bfloat16)
    gproj[1] = (grad_dense * conv_out).astype(jnp.bfloat16)
    gproj[2] = (grad_source * gate_in).astype(jnp.bfloat16)
    gfilt[...] = of_filter

    each(0, z, lambda other: along_z(other).wait_send())
    each(z + 1, nz, lambda other: along_z(other).wait_send())
    for place, step in events:
        if step:
            ring(0, place, step).wait_send()
            ring(1, place, step).wait_send()
    for kind in (filters, signals, results):
        for step in others:
            kind(step).wait_send()


def per_device(tokens, in_weight, long_filter, grad_out):
    rows, width = long_filter.shape
    depth = in_weight.shape[0]
    nseq = lax.axis_size("seq")
    ny, nz = grid_of(lax.axis_size("chan"))
    per = width // nseq
    forward, inverse = tables(rows)
    vmem = pl.BlockSpec(memory_space=pltpu.VMEM)
    hbm = pl.BlockSpec(memory_space=pltpu.HBM)
    bf16, f32 = jnp.bfloat16, jnp.float32
    dma = pltpu.SemaphoreType.DMA
    gated_out, grad_proj, grad_filter = pl.pallas_call(
        functools.partial(body, ny, nz, nseq),
        name="gather_project_convolve",
        out_shape=(
            jax.ShapeDtypeStruct((rows, width), bf16),
            jax.ShapeDtypeStruct((3, rows, width), bf16),
            jax.ShapeDtypeStruct((rows, width), f32),
        ),
        in_specs=[hbm] * 6,
        out_specs=(vmem, vmem, vmem),
        scratch_shapes=[
            pltpu.VMEM((rows, width), f32),
            pltpu.VMEM((rows, width), bf16),
            pltpu.VMEM((depth, 3 * width), bf16),
            pltpu.VMEM(forward.shape, bf16),
            pltpu.VMEM(inverse.shape, bf16),
            pltpu.VMEM((nz, ny, rows, width), bf16),
            pltpu.VMEM((rows, 3 * width), f32),
            pltpu.VMEM((nseq, per, rows), f32),
            pltpu.VMEM((nseq, per, rows), f32),
            pltpu.VMEM((nseq, per, 2 * rows), f32),
            pltpu.VMEM((nseq, 2 * per, rows), bf16),
            pltpu.VMEM((nseq, 2 * per, rows), bf16),
            pltpu.VMEM((nseq, 2 * per, 2 * rows), f32),
            pltpu.VMEM((nseq, 3 * per, 2 * rows), f32),
            pltpu.VMEM((nseq, 3 * per, rows), bf16),
            pltpu.VMEM((nseq, 3 * per, rows), bf16),
            dma((8,)),
            dma((nz,)),
            dma((nz,)),
            dma((2, nz, ny // 2 + 1)),
            dma((2, nz, ny // 2 + 1)),
            dma((nseq,)),
            dma((nseq,)),
            dma((nseq,)),
            dma((nseq,)),
            dma((nseq,)),
            dma((nseq,)),
        ],
        compiler_params=pltpu.CompilerParams(
            collective_id=0, has_side_effects=True, vmem_limit_bytes=40 * 2**20
        ),
    )(
        *(
            pltpu.with_memory_space_constraint(operand, pltpu.HBM)
            for operand in (
                tokens,
                jnp.transpose(in_weight, (1, 0, 2)),
                long_filter,
                grad_out,
                jnp.asarray(forward),
                jnp.asarray(inverse),
            )
        )
    )
    return gated_out, jnp.transpose(grad_proj, (1, 0, 2)), grad_filter


def solution(mesh):
    in_specs = (P("seq", "chan"), P(None, None, "chan"), P("seq", "chan"), P("seq", "chan"))
    out_specs = (P("seq", "chan"), P("seq", None, "chan"), P("seq", "chan"))
    return jax.shard_map(
        per_device, mesh=mesh, in_specs=in_specs, out_specs=out_specs, check_vma=False
    )
```

```python
import functools
import math

import jax
import jax.numpy as jnp
import ml_dtypes
import numpy as np
from jax import lax
from jax.experimental import pallas as pl
from jax.experimental.pallas import tpu as pltpu
from jax.sharding import PartitionSpec as P

MESH = pl.DeviceIdType.MESH
EARLY = (
    (0, 0), (0, 1), (1, 0), (0, 2), (2, 0), (1, 1), (0, 3), (2, 1),
    (3, 0), (1, 2), (0, 4), (2, 2), (3, 1), (1, 3), (4, 0), (5, 0),
    (6, 0), (7, 0), (3, 2), (2, 3), (4, 1), (1, 4), (5, 1), (6, 1),
    (7, 1), (3, 3), (2, 4), (4, 2), (5, 2), (6, 2), (7, 2), (3, 4),
    (4, 3), (5, 3), (6, 3), (7, 3), (4, 4), (5, 4), (6, 4), (7, 4),
)
LATE = (
    (0, 0), (0, 1), (0, 2), (7, 0), (6, 0), (5, 0), (1, 0), (4, 0),
    (7, 1), (2, 0), (6, 1), (5, 1), (0, 3), (1, 1), (3, 0), (4, 1),
    (7, 2), (2, 1), (6, 2), (5, 2), (0, 4), (1, 2), (3, 1), (4, 2),
    (7, 3), (2, 2), (6, 3), (5, 3), (1, 3), (3, 2), (4, 3), (7, 4),
    (2, 3), (6, 4), (5, 4), (1, 4), (3, 3), (4, 4), (2, 4), (3, 4),
)


def grid_of(chans):
    columns = 1
    while columns * columns < chans:
        columns *= 2
    return chans // columns, columns


def split_table(table):
    high = table.astype(ml_dtypes.bfloat16)
    low = (table - high.astype(np.float64)).astype(ml_dtypes.bfloat16)
    return high, low


def tables(rows):
    angle = math.pi * np.outer(np.arange(2 * rows), 2 * np.arange(rows) + 1) / (2 * rows)
    forward = np.concatenate([np.cos(angle), -np.sin(angle)], axis=1)[:rows]
    inverse = np.concatenate([np.cos(angle), -np.sin(angle)], axis=1).T / rows
    return np.concatenate(split_table(forward), axis=0), np.stack(split_table(inverse))


def dot(left, right):
    return jnp.dot(left, right, preferred_element_type=jnp.float32)


def split(value):
    high = value.astype(jnp.bfloat16)
    return high, (value - high.astype(jnp.float32)).astype(jnp.bfloat16)


def body(
    ny, nz, nseq,
    tok_hbm, w_hbm, filt_hbm, gout_hbm, fwd_hbm, inv_hbm,
    gated, gproj, gfilt,
    filt, gout, w, fwd, inv, tokens, acc,
    fsend, frecv, fspec, xsend, xrecv, xspec, prod, ysend, yrecv,
    local_sem, z_send, z_recv, ring_send, ring_recv, f_send, f_recv, x_send, x_recv, y_send, y_recv,
):
    rows, width = filt.shape
    half = rows // 2
    per = width // nseq
    seq = lax.axis_index("seq")
    chan = lax.axis_index("chan")
    y, z = chan // nz, chan % nz

    weights = [
        pltpu.make_async_copy(w_hbm.at[b], w.at[:, pl.ds(b * width, width)], local_sem.at[b])
        for b in range(3)
    ]
    constants = [
        pltpu.make_async_copy(fwd_hbm, fwd, local_sem.at[3]),
        pltpu.make_async_copy(inv_hbm, inv, local_sem.at[4]),
    ]
    inputs = [
        pltpu.make_async_copy(tok_hbm, tokens.at[z, y], local_sem.at[5]),
        pltpu.make_async_copy(filt_hbm, filt, local_sem.at[6]),
        pltpu.make_async_copy(gout_hbm, gout, local_sem.at[7]),
    ]
    for copy in inputs + constants + weights:
        copy.start()

    barrier = pltpu.get_barrier_semaphore()
    up, down = (seq, lax.rem(y + 1, ny) * nz + z), (seq, lax.rem(y + ny - 1, ny) * nz + z)

    def greet(peer):
        pl.semaphore_signal(barrier, inc=1, device_id=peer, device_id_type=MESH)

    def each(first, last, action):
        def step_of(step, carry):
            action(step)
            return carry
        lax.fori_loop(first, last, step_of, 0)

    greet(up)
    greet(down)

    def rank(column):
        return column + jnp.where((column == 0) & (y == 0) & (seq == 0), nz, 0)

    def if_rank(higher, action):
        def of_other(step):
            other = lax.rem(z + step, nz)

            @pl.when(rank(other) > rank(z) if higher else rank(other) < rank(z))
            def _():
                action(other)
        each(1, nz, of_other)

    if_rank(True, lambda other: greet((seq, y * nz + other)))

    @pl.when(seq != 0)
    def _():
        each(1, nseq, lambda step: greet((lax.rem(seq + step, nseq), chan)))

    for copy in inputs:
        copy.wait()
    fsend[...] = filt[...].T.reshape(nseq, per, rows)
    frecv[seq] = fsend[seq]
    acc[...] = jnp.zeros_like(acc)
    lower = jnp.where((y == 0) & (seq == 0), jnp.where(z == 0, nz - 1, z - 1), z)
    pl.semaphore_wait(barrier, 2 + lower + jnp.where(seq == 0, nseq - 1, nseq - 2))

    def along_z(other):
        return pltpu.make_async_remote_copy(
            tokens.at[z, y], tokens.at[z, y], z_send.at[other], z_recv.at[z],
            device_id=(seq, y * nz + other), device_id_type=MESH,
        )

    def from_z(other):
        return pltpu.make_async_remote_copy(
            tokens.at[other, y], tokens.at[other, y], z_send.at[other], z_recv.at[other],
            device_id=(seq, y * nz + other), device_id_type=MESH,
        )

    def column(place):
        if place == 0:
            return z
        later = jnp.where(place < z, place, place + 1)
        return jnp.where(z == 0, place, 0 if place == nz - 1 else later)

    columns = [column(place) for place in range(nz)]

    last = ny // 2
    rows_up = [lax.rem(y + ny - step, ny) for step in range(last + 1)]
    rows_down = [lax.rem(y + step, ny) for step in range(last + 1)]

    def ring(way, place, step, arriving=False):
        chunk = (rows_up, rows_down)[way][step if arriving else step - 1]
        block = tokens.at[columns[place], chunk]
        if step == last:
            block = block.at[pl.ds(way * half, half)]
        return pltpu.make_async_remote_copy(
            block, block, ring_send.at[way, place, step], ring_recv.at[way, place, step],
            device_id=(up, down)[way], device_id_type=MESH,
        )

    def multiply(place, chunks):
        left = [tokens[columns[place], chunk] for chunk in chunks]
        right = [
            w[pl.ds(pl.multiple_of((chunk * nz + columns[place]) * width, width), width)]
            for chunk in chunks
        ]
        acc[...] += dot(jnp.concatenate(left, axis=1), jnp.concatenate(right, axis=0))

    def exchange(source, target, send, recv, step):
        to = lax.rem(seq + step, nseq)
        return pltpu.make_async_remote_copy(
            source.at[to], target.at[seq], send.at[step], recv.at[step],
            device_id=(to, chan), device_id_type=MESH,
        )

    others = sorted(range(1, nseq), key=lambda step: abs(step - nseq // 2))
    filters = functools.partial(exchange, fsend, frecv, f_send, f_recv)
    signals = functools.partial(exchange, xsend, xrecv, x_send, x_recv)
    results = functools.partial(exchange, ysend, yrecv, y_send, y_recv)

    if_rank(False, lambda other: along_z(other).start())

    def first_filters(step):
        @pl.when(lax.rem(seq + step, nseq) != 0)
        def _():
            filters(step).start()

    def other_filters(step):
        @pl.when(step != seq)
        def _():
            filters(step).wait_recv()

    events = sorted(
        ((place, step) for place in range(nz) for step in range(last + 1)),
        key=lambda event: (event[0] + event[1], event[0]),
    )

    def take(order):
        for position, (place, step) in enumerate(order):
            if step == 0 and place > 0:
                from_z(columns[place]).wait_recv()

                @pl.when(rank(columns[place]) > rank(z))
                def _(place=place):
                    along_z(columns[place]).start()

            if step > 0:
                ring(0, place, step, arriving=True).wait_recv()
                ring(1, place, step, arriving=True).wait_recv()
            if step < last:
                ring(0, place, step + 1).start()
                ring(1, place, step + 1).start()
            if position == 0:
                each(1, nseq, first_filters)
                for copy in weights:
                    copy.wait()
            if step in (0, last):
                multiply(place, [rows_up[step]])
            else:
                multiply(place, [rows_up[step], rows_down[step]])
            if position == len(order) // 2:
                @pl.when(seq != 0)
                def _():
                    filters(seq).wait_recv()
                    filters(nseq - seq).start()

    known = (ny, nz) == (8, 8)

    @pl.when(z < nz // 2)
    def _():
        take(EARLY if known else events)

    @pl.when(z >= nz // 2)
    def _():
        take(LATE if known else events)

    projection = acc[...].astype(jnp.bfloat16).astype(jnp.float32)
    gate_in, gate_out, values = (projection[:, b * width : (b + 1) * width] for b in range(3))
    grad_dense = gout[...].astype(jnp.float32)
    source = (gate_in * values).T.reshape(nseq, per, rows)
    grad_conv = (grad_dense * gate_out).T.reshape(nseq, per, rows)
    xsend[...] = jnp.concatenate([source, grad_conv], axis=1).astype(jnp.bfloat16)
    for step in others:
        signals(step).start()
    xrecv[seq] = xsend[seq]

    each(1, nseq, other_filters)
    for copy in constants:
        copy.wait()
    high, low = split(frecv[...].reshape(nseq * per, rows))
    fspec[...] = (
        dot(jnp.concatenate([high, high], axis=1), fwd[...]) + dot(low, fwd[:rows])
    ).reshape(nseq, per, 2 * rows)

    for step in others:
        signals(step).wait_recv()

    received = xrecv[...].reshape(nseq * 2 * per, rows)
    xspec[...] = dot(jnp.concatenate([received, received], axis=1), fwd[...]).reshape(
        nseq, 2 * per, 2 * rows
    )

    def spectrum(ref, block, first_row):
        return (
            ref[block, first_row : first_row + per, :rows],
            ref[block, first_row : first_row + per, rows:],
        )

    for out in range(nseq):
        re, im = 0.0, 0.0
        for j in range(out + 1):
            f_re, f_im = spectrum(fspec, j, 0)
            s_re, s_im = spectrum(xspec, out - j, 0)
            re = re + (f_re * s_re - f_im * s_im)
            im = im + (f_re * s_im + f_im * s_re)
        prod[out, :per, :rows] = re
        prod[out, :per, rows:] = im
        re, im, re2, im2 = 0.0, 0.0, 0.0, 0.0
        for j in range(nseq - out):
            g_re, g_im = spectrum(xspec, out + j, per)
            f_re, f_im = spectrum(fspec, j, 0)
            s_re, s_im = spectrum(xspec, j, 0)
            re = re + (f_re * g_re + f_im * g_im)
            im = im + (f_re * g_im - f_im * g_re)
            re2 = re2 + (s_re * g_re + s_im * g_im)
            im2 = im2 + (s_re * g_im - s_im * g_re)
        prod[out, per : 2 * per, :rows] = re
        prod[out, per : 2 * per, rows:] = im
        prod[out, 2 * per :, :rows] = re2
        prod[out, 2 * per :, rows:] = im2

    high, low = split(prod[...].reshape(nseq * 3 * per, 2 * rows))
    prod[...] = (dot(high, inv[0]) + dot(low, inv[0]) + dot(high, inv[1])).reshape(
        nseq, 3 * per, 2 * rows
    )
    for block in range(nseq):
        conv = prod[block, :per, :rows]
        grads = prod[block, per:, :rows]
        if block > 0:
            conv = conv + prod[block - 1, :per, rows:]
        if block < nseq - 1:
            grads = grads - prod[block + 1, per:, rows:]
        ysend[block] = jnp.concatenate([conv, grads], axis=0).astype(jnp.bfloat16)
    for step in others:
        results(step).start()
    yrecv[seq] = ysend[seq]
    for step in others:
        results(step).wait_recv()

    back = yrecv[...].astype(jnp.float32)
    conv_out = back[:, :per].reshape(width, rows).T
    grad_source = back[:, per : 2 * per].reshape(width, rows).T
    of_filter = back[:, 2 * per :].reshape(width, rows).T
    gated[...] = (gate_out * conv_out).astype(jnp.bfloat16)
    gproj[0] = (grad_source * values).astype(jnp.bfloat16)
    gproj[1] = (grad_dense * conv_out).astype(jnp.bfloat16)
    gproj[2] = (grad_source * gate_in).astype(jnp.bfloat16)
    gfilt[...] = of_filter

    each(0, z, lambda other: along_z(other).wait_send())
    each(z + 1, nz, lambda other: along_z(other).wait_send())
    for place, step in events:
        if step:
            ring(0, place, step).wait_send()
            ring(1, place, step).wait_send()
    for kind in (filters, signals, results):
        for step in others:
            kind(step).wait_send()


def per_device(tokens, in_weight, long_filter, grad_out):
    rows, width = long_filter.shape
    depth = in_weight.shape[0]
    nseq = lax.axis_size("seq")
    ny, nz = grid_of(lax.axis_size("chan"))
    per = width // nseq
    forward, inverse = tables(rows)
    vmem = pl.BlockSpec(memory_space=pltpu.VMEM)
    hbm = pl.BlockSpec(memory_space=pltpu.HBM)
    bf16, f32 = jnp.bfloat16, jnp.float32
    dma = pltpu.SemaphoreType.DMA
    gated_out, grad_proj, grad_filter = pl.pallas_call(
        functools.partial(body, ny, nz, nseq),
        name="gather_project_convolve",
        out_shape=(
            jax.ShapeDtypeStruct((rows, width), bf16),
            jax.ShapeDtypeStruct((3, rows, width), bf16),
            jax.ShapeDtypeStruct((rows, width), f32),
        ),
        in_specs=[hbm] * 6,
        out_specs=(vmem, vmem, vmem),
        scratch_shapes=[
            pltpu.VMEM((rows, width), f32),
            pltpu.VMEM((rows, width), bf16),
            pltpu.VMEM((depth, 3 * width), bf16),
            pltpu.VMEM(forward.shape, bf16),
            pltpu.VMEM(inverse.shape, bf16),
            pltpu.VMEM((nz, ny, rows, width), bf16),
            pltpu.VMEM((rows, 3 * width), f32),
            pltpu.VMEM((nseq, per, rows), f32),
            pltpu.VMEM((nseq, per, rows), f32),
            pltpu.VMEM((nseq, per, 2 * rows), f32),
            pltpu.VMEM((nseq, 2 * per, rows), bf16),
            pltpu.VMEM((nseq, 2 * per, rows), bf16),
            pltpu.VMEM((nseq, 2 * per, 2 * rows), f32),
            pltpu.VMEM((nseq, 3 * per, 2 * rows), f32),
            pltpu.VMEM((nseq, 3 * per, rows), bf16),
            pltpu.VMEM((nseq, 3 * per, rows), bf16),
            dma((8,)),
            dma((nz,)),
            dma((nz,)),
            dma((2, nz, ny // 2 + 1)),
            dma((2, nz, ny // 2 + 1)),
            dma((nseq,)),
            dma((nseq,)),
            dma((nseq,)),
            dma((nseq,)),
            dma((nseq,)),
            dma((nseq,)),
        ],
        compiler_params=pltpu.CompilerParams(
            collective_id=0, has_side_effects=True, vmem_limit_bytes=40 * 2**20
        ),
    )(
        *(
            pltpu.with_memory_space_constraint(operand, pltpu.HBM)
            for operand in (
                tokens,
                jnp.transpose(in_weight, (1, 0, 2)),
                long_filter,
                grad_out,
                jnp.asarray(forward),
                jnp.asarray(inverse),
            )
        )
    )
    return gated_out, jnp.transpose(grad_proj, (1, 0, 2)), grad_filter


def solution(mesh):
    in_specs = (P("seq", "chan"), P(None, None, "chan"), P("seq", "chan"), P("seq", "chan"))
    out_specs = (P("seq", "chan"), P("seq", None, "chan"), P("seq", "chan"))
    return jax.shard_map(
        per_device, mesh=mesh, in_specs=in_specs, out_specs=out_specs, check_vma=False
    )
```

```python
import functools
import math

import jax
import jax.numpy as jnp
import ml_dtypes
import numpy as np
from jax import lax
from jax.experimental import pallas as pl
from jax.experimental.pallas import tpu as pltpu
from jax.sharding import PartitionSpec as P

MESH = pl.DeviceIdType.MESH
PIECES = 2
KEY = 3


def by_distance(count):
    return sorted(range(count), key=lambda offset: (min(offset, count - offset), offset))


def grid_of(chans):
    columns = 1
    while columns * columns < chans:
        columns *= 2
    return chans // columns, columns


def split_table(table):
    high = table.astype(ml_dtypes.bfloat16)
    low = (table - high.astype(np.float64)).astype(ml_dtypes.bfloat16)
    return high, low


def tables(rows):
    angle = math.pi * np.outer(np.arange(2 * rows), 2 * np.arange(rows) + 1) / (2 * rows)
    forward = np.concatenate([np.cos(angle), -np.sin(angle)], axis=1)[:rows]
    inverse = np.concatenate([np.cos(angle), -np.sin(angle)], axis=1).T / rows
    return np.concatenate(split_table(forward), axis=0), np.stack(split_table(inverse))


def dot(left, right):
    return jnp.dot(left, right, preferred_element_type=jnp.float32)


def split(value):
    high = value.astype(jnp.bfloat16)
    return high, (value - high.astype(jnp.float32)).astype(jnp.bfloat16)


def body(
    ny, nz, nseq,
    tok_hbm, w_hbm, filt_hbm, gout_hbm, fwd_hbm, inv_hbm,
    gated, gproj, gfilt,
    tok, filt, gout, w, fwd, inv, abuf, bbuf, acc,
    fsend, frecv, fspec, xsend, xrecv, xspec, prod, ysend, yrecv,
    local_sem, p1_send, p1_recv, ring_send, ring_recv, f_send, f_recv, x_send, x_recv, y_send, y_recv,
):
    rows, width = filt.shape
    half = rows // 2
    per = width // nseq
    seq = lax.axis_index("seq")
    chan = lax.axis_index("chan")
    y, z = chan // nz, chan % nz

    weights = [
        pltpu.make_async_copy(w_hbm.at[b], w.at[:, pl.ds(b * width, width)], local_sem.at[b])
        for b in range(3)
    ]
    constants = [
        pltpu.make_async_copy(fwd_hbm, fwd, local_sem.at[3]),
        pltpu.make_async_copy(inv_hbm, inv, local_sem.at[4]),
    ]
    inputs = [
        pltpu.make_async_copy(tok_hbm, tok, local_sem.at[5]),
        pltpu.make_async_copy(filt_hbm, filt, local_sem.at[6]),
        pltpu.make_async_copy(gout_hbm, gout, local_sem.at[7]),
    ]
    for copy in inputs + constants + weights:
        copy.start()

    barrier = pltpu.get_barrier_semaphore()

    def seq_peer(step):
        return (lax.rem(seq + step, nseq), chan)

    def z_peer(step):
        return (seq, y * nz + lax.rem(z + step, nz))

    def y_peer(step):
        return (seq, lax.rem(y + step, ny) * nz + z)

    def greet(peer):
        pl.semaphore_signal(barrier, inc=1, device_id=peer, device_id_type=MESH)

    def each(first, last, action):
        def step_of(step, carry):
            action(step)
            return carry
        lax.fori_loop(first, last, step_of, 0)

    at_head = (y == 0) & (seq == 0)

    def rank(column):
        return column + jnp.where((column == 0) & at_head, nz, 0)

    each(1, ny, lambda step: greet(y_peer(step)))

    def greet_higher(step):
        other = lax.rem(z + step, nz)

        @pl.when(rank(other) > rank(z))
        def _():
            greet((seq, y * nz + other))

    each(1, nz, greet_higher)

    @pl.when(seq != 0)
    def _():
        each(1, nseq, lambda step: greet(seq_peer(step)))

    inputs[0].wait()
    slots_y, slots_z = by_distance(ny), by_distance(nz)
    abuf[y, 0] = tok[:half]
    bbuf[z, 0] = tok[half:]
    lower = jnp.where(at_head, jnp.where(z == 0, nz - 1, z - 1), z)
    pl.semaphore_wait(barrier, ny - 1 + lower + jnp.where(seq == 0, nseq - 1, nseq - 2))

    def first(which, slot):
        slots, source = (slots_z, tok.at[pl.ds(0, half)]) if which == 0 else (slots_y, tok.at[pl.ds(half, half)])
        target = (abuf.at[y] if which == 0 else bbuf.at[z]).at[slot]
        return pltpu.make_async_remote_copy(
            source, target, p1_send.at[which, slot], p1_recv.at[which, slot],
            device_id=(z_peer if which == 0 else y_peer)(len(slots) - slots[slot]), device_id_type=MESH,
        )

    steps = [ny // 2, ny // 2, nz // 2, nz // 2]
    hops = [y_peer(1), y_peer(ny - 1), z_peer(1), z_peer(nz - 1)]
    chunks = [
        [
            lax.rem(place + count - sign * step, count) if step else place
            for step in range(count // 2 + 1)
        ]
        for place, count, sign in ((y, ny, 1), (y, ny, -1), (z, nz, 1), (z, nz, -1))
    ]
    size = [(nz if direction < 2 else ny) // PIECES for direction in range(4)]

    def ring(direction, step, piece, arriving=False):
        buffer = abuf if direction < 2 else bbuf
        chunk = chunks[direction][step if arriving else step - 1]
        block = buffer.at[chunk, pl.ds(piece * size[direction], size[direction])]
        return pltpu.make_async_remote_copy(
            block, block, ring_send.at[direction, step, piece], ring_recv.at[direction, step, piece],
            device_id=hops[direction], device_id_type=MESH,
        )

    def sends(direction, step, piece):
        last = steps[direction]
        return step < last or (step == last and piece % 2 == direction % 2)

    def multiply(direction, chunk, piece):
        count, first_slot = size[direction], piece * size[direction]
        buffer, out = (abuf, pl.ds(0, half)) if direction < 2 else (bbuf, pl.ds(half, half))
        left = jnp.concatenate([buffer[chunk, first_slot + i] for i in range(count)], axis=1)
        right = []
        for i in range(count):
            if direction < 2:
                block = chunk * nz + lax.rem(z + slots_z[first_slot + i], nz)
            else:
                block = lax.rem(y + slots_y[first_slot + i], ny) * nz + chunk
            right.append(w[pl.ds(pl.multiple_of(block * width, width), width)])
        acc[out] += dot(left, jnp.concatenate(right, axis=0))

    def exchange(source, target, send, recv, step):
        to = lax.rem(seq + step, nseq)
        return pltpu.make_async_remote_copy(
            source.at[to], target.at[seq], send.at[step], recv.at[step],
            device_id=(to, chan), device_id_type=MESH,
        )

    others = sorted(range(1, nseq), key=lambda step: abs(step - nseq // 2))
    filters = functools.partial(exchange, fsend, frecv, f_send, f_recv)
    signals = functools.partial(exchange, xsend, xrecv, x_send, x_recv)
    results = functools.partial(exchange, ysend, yrecv, y_send, y_recv)

    for slot in range(1, max(ny, nz)):
        for which, count in ((0, nz), (1, ny)):
            if slot < count and which:
                first(which, slot).start()
            elif slot < count:
                @pl.when(rank(lax.rem(z + nz - slots_z[slot], nz)) < rank(z))
                def _(slot=slot):
                    first(0, slot).start()

    for copy in inputs[1:]:
        copy.wait()
    fsend[...] = filt[...].T.reshape(nseq, per, rows)

    def first_filters(step):
        @pl.when(lax.rem(seq + step, nseq) != 0)
        def _():
            filters(step).start()

    def other_filters(step):
        @pl.when(step != seq)
        def _():
            filters(step).wait_recv()

    each(1, nseq, first_filters)
    frecv[seq] = fsend[seq]
    acc[...] = jnp.zeros_like(acc)

    events = sorted(
        ((step, piece) for step in range(max(steps) + 1) for piece in range(PIECES)),
        key=lambda event: (KEY * event[0] + event[1], event[0]),
    )
    ready = False
    for step, piece in events:
        arrived = []
        for direction in range(4):
            if step == 0:
                if direction % 2 == 0:
                    for slot in range(piece * size[direction], (piece + 1) * size[direction]):
                        if slot:
                            first(direction // 2, slot).wait_recv()
                        if slot and direction == 0:
                            back = slots_z.index(nz - slots_z[slot])

                            @pl.when(rank(lax.rem(z + slots_z[slot], nz)) > rank(z))
                            def _(back=back):
                                first(0, back).start()

                    arrived.append(direction)
            elif sends(direction, step, piece):
                ring(direction, step, piece, arriving=True).wait_recv()
                arrived.append(direction)
            if (step == 0 or direction in arrived) and sends(direction, step + 1, piece):
                ring(direction, step + 1, piece).start()
        if not ready:
            for copy in weights:
                copy.wait()
            ready = True
        for direction in arrived:
            multiply(direction, chunks[direction][step], piece)

    @pl.when(seq != 0)
    def _():
        filters(seq).wait_recv()
        filters(nseq - seq).start()

    projection = acc[...].astype(jnp.bfloat16).astype(jnp.float32)
    gate_in, gate_out, values = (projection[:, b * width : (b + 1) * width] for b in range(3))
    grad_dense = gout[...].astype(jnp.float32)
    source = (gate_in * values).T.reshape(nseq, per, rows)
    grad_conv = (grad_dense * gate_out).T.reshape(nseq, per, rows)
    xsend[...] = jnp.concatenate([source, grad_conv], axis=1).astype(jnp.bfloat16)
    for step in others:
        signals(step).start()
    xrecv[seq] = xsend[seq]

    each(1, nseq, other_filters)
    for copy in constants:
        copy.wait()
    high, low = split(frecv[...].reshape(nseq * per, rows))
    fspec[...] = (
        dot(jnp.concatenate([high, high], axis=1), fwd[...]) + dot(low, fwd[:rows])
    ).reshape(nseq, per, 2 * rows)

    for step in others:
        signals(step).wait_recv()

    received = xrecv[...].reshape(nseq * 2 * per, rows)
    xspec[...] = dot(jnp.concatenate([received, received], axis=1), fwd[...]).reshape(
        nseq, 2 * per, 2 * rows
    )

    def spectrum(ref, block, first_row):
        return (
            ref[block, first_row : first_row + per, :rows],
            ref[block, first_row : first_row + per, rows:],
        )

    for out in range(nseq):
        re, im = 0.0, 0.0
        for j in range(out + 1):
            f_re, f_im = spectrum(fspec, j, 0)
            s_re, s_im = spectrum(xspec, out - j, 0)
            re = re + (f_re * s_re - f_im * s_im)
            im = im + (f_re * s_im + f_im * s_re)
        prod[out, :per, :rows] = re
        prod[out, :per, rows:] = im
        re, im, re2, im2 = 0.0, 0.0, 0.0, 0.0
        for j in range(nseq - out):
            g_re, g_im = spectrum(xspec, out + j, per)
            f_re, f_im = spectrum(fspec, j, 0)
            s_re, s_im = spectrum(xspec, j, 0)
            re = re + (f_re * g_re + f_im * g_im)
            im = im + (f_re * g_im - f_im * g_re)
            re2 = re2 + (s_re * g_re + s_im * g_im)
            im2 = im2 + (s_re * g_im - s_im * g_re)
        prod[out, per : 2 * per, :rows] = re
        prod[out, per : 2 * per, rows:] = im
        prod[out, 2 * per :, :rows] = re2
        prod[out, 2 * per :, rows:] = im2

    high, low = split(prod[...].reshape(nseq * 3 * per, 2 * rows))
    prod[...] = (dot(high, inv[0]) + dot(low, inv[0]) + dot(high, inv[1])).reshape(
        nseq, 3 * per, 2 * rows
    )
    for block in range(nseq):
        conv = prod[block, :per, :rows]
        grads = prod[block, per:, :rows]
        if block > 0:
            conv = conv + prod[block - 1, :per, rows:]
        if block < nseq - 1:
            grads = grads - prod[block + 1, per:, rows:]
        ysend[block] = jnp.concatenate([conv, grads], axis=0).astype(jnp.bfloat16)
    for step in others:
        results(step).start()
    yrecv[seq] = ysend[seq]
    for step in others:
        results(step).wait_recv()

    back = yrecv[...].astype(jnp.float32)
    conv_out = back[:, :per].reshape(width, rows).T
    grad_source = back[:, per : 2 * per].reshape(width, rows).T
    of_filter = back[:, 2 * per :].reshape(width, rows).T
    gated[...] = (gate_out * conv_out).astype(jnp.bfloat16)
    gproj[0] = (grad_source * values).astype(jnp.bfloat16)
    gproj[1] = (grad_dense * conv_out).astype(jnp.bfloat16)
    gproj[2] = (grad_source * gate_in).astype(jnp.bfloat16)
    gfilt[...] = of_filter

    for which, count in ((0, nz), (1, ny)):
        for slot in range(1, count):
            first(which, slot).wait_send()
    for step, piece in events:
        for direction in range(4):
            if step and sends(direction, step, piece):
                ring(direction, step, piece).wait_send()
    for kind in (filters, signals, results):
        for step in others:
            kind(step).wait_send()


def per_device(tokens, in_weight, long_filter, grad_out):
    rows, width = long_filter.shape
    depth = in_weight.shape[0]
    nseq = lax.axis_size("seq")
    ny, nz = grid_of(lax.axis_size("chan"))
    per = width // nseq
    forward, inverse = tables(rows)
    vmem = pl.BlockSpec(memory_space=pltpu.VMEM)
    hbm = pl.BlockSpec(memory_space=pltpu.HBM)
    bf16, f32 = jnp.bfloat16, jnp.float32
    dma = pltpu.SemaphoreType.DMA
    steps = max(ny, nz) // 2 + 1
    gated_out, grad_proj, grad_filter = pl.pallas_call(
        functools.partial(body, ny, nz, nseq),
        name="gather_project_convolve",
        out_shape=(
            jax.ShapeDtypeStruct((rows, width), bf16),
            jax.ShapeDtypeStruct((3, rows, width), bf16),
            jax.ShapeDtypeStruct((rows, width), f32),
        ),
        in_specs=[hbm] * 6,
        out_specs=(vmem, vmem, vmem),
        scratch_shapes=[
            pltpu.VMEM((rows, width), bf16),
            pltpu.VMEM((rows, width), f32),
            pltpu.VMEM((rows, width), bf16),
            pltpu.VMEM((depth, 3 * width), bf16),
            pltpu.VMEM(forward.shape, bf16),
            pltpu.VMEM(inverse.shape, bf16),
            pltpu.VMEM((ny, nz, rows // 2, width), bf16),
            pltpu.VMEM((nz, ny, rows // 2, width), bf16),
            pltpu.VMEM((rows, 3 * width), f32),
            pltpu.VMEM((nseq, per, rows), f32),
            pltpu.VMEM((nseq, per, rows), f32),
            pltpu.VMEM((nseq, per, 2 * rows), f32),
            pltpu.VMEM((nseq, 2 * per, rows), bf16),
            pltpu.VMEM((nseq, 2 * per, rows), bf16),
            pltpu.VMEM((nseq, 2 * per, 2 * rows), f32),
            pltpu.VMEM((nseq, 3 * per, 2 * rows), f32),
            pltpu.VMEM((nseq, 3 * per, rows), bf16),
            pltpu.VMEM((nseq, 3 * per, rows), bf16),
            dma((8,)),
            dma((2, max(ny, nz))),
            dma((2, max(ny, nz))),
            dma((4, steps, PIECES)),
            dma((4, steps, PIECES)),
            dma((nseq,)),
            dma((nseq,)),
            dma((nseq,)),
            dma((nseq,)),
            dma((nseq,)),
            dma((nseq,)),
        ],
        compiler_params=pltpu.CompilerParams(
            collective_id=0, has_side_effects=True, vmem_limit_bytes=40 * 2**20
        ),
    )(
        *(
            pltpu.with_memory_space_constraint(operand, pltpu.HBM)
            for operand in (
                tokens,
                jnp.transpose(in_weight, (1, 0, 2)),
                long_filter,
                grad_out,
                jnp.asarray(forward),
                jnp.asarray(inverse),
            )
        )
    )
    return gated_out, jnp.transpose(grad_proj, (1, 0, 2)), grad_filter


def solution(mesh):
    in_specs = (P("seq", "chan"), P(None, None, "chan"), P("seq", "chan"), P("seq", "chan"))
    out_specs = (P("seq", "chan"), P("seq", None, "chan"), P("seq", "chan"))
    return jax.shard_map(
        per_device, mesh=mesh, in_specs=in_specs, out_specs=out_specs, check_vma=False
    )
```

```python
import functools
import math

import jax
import jax.numpy as jnp
import ml_dtypes
import numpy as np
from jax import lax
from jax.experimental import pallas as pl
from jax.experimental.pallas import tpu as pltpu
from jax.sharding import PartitionSpec as P

MESH = pl.DeviceIdType.MESH
PIECES = 2
KEY = 3


def by_distance(count):
    return sorted(range(count), key=lambda offset: (min(offset, count - offset), offset))


def grid_of(chans):
    columns = 1
    while columns * columns < chans:
        columns *= 2
    return chans // columns, columns


def split_table(table):
    high = table.astype(ml_dtypes.bfloat16)
    low = (table - high.astype(np.float64)).astype(ml_dtypes.bfloat16)
    return high, low


def tables(rows):
    angle = math.pi * np.outer(np.arange(2 * rows), 2 * np.arange(rows) + 1) / (2 * rows)
    forward = np.concatenate([np.cos(angle), -np.sin(angle)], axis=1)[:rows]
    inverse = np.concatenate([np.cos(angle), -np.sin(angle)], axis=1).T / rows
    return np.concatenate(split_table(forward), axis=0), np.stack(split_table(inverse))


def dot(left, right):
    return jnp.dot(left, right, preferred_element_type=jnp.float32)


def split(value):
    high = value.astype(jnp.bfloat16)
    return high, (value - high.astype(jnp.float32)).astype(jnp.bfloat16)


def body(
    ny, nz, nseq,
    tok_hbm, w_hbm, filt_hbm, gout_hbm, fwd_hbm, inv_hbm,
    gated, gproj, gfilt,
    tok, filt, gout, w, fwd, inv, abuf, bbuf, acc,
    fsend, frecv, fspec, xsend, xrecv, xspec, prod, ysend, yrecv,
    local_sem, p1_send, p1_recv, ring_send, ring_recv, f_send, f_recv, x_send, x_recv, y_send, y_recv,
):
    rows, width = filt.shape
    half = rows // 2
    per = width // nseq
    seq = lax.axis_index("seq")
    chan = lax.axis_index("chan")
    y, z = chan // nz, chan % nz

    weights = [
        pltpu.make_async_copy(w_hbm.at[b], w.at[:, pl.ds(b * width, width)], local_sem.at[b])
        for b in range(3)
    ]
    constants = [
        pltpu.make_async_copy(fwd_hbm, fwd, local_sem.at[3]),
        pltpu.make_async_copy(inv_hbm, inv, local_sem.at[4]),
    ]
    inputs = [
        pltpu.make_async_copy(tok_hbm, tok, local_sem.at[5]),
        pltpu.make_async_copy(filt_hbm, filt, local_sem.at[6]),
        pltpu.make_async_copy(gout_hbm, gout, local_sem.at[7]),
    ]
    for copy in inputs + constants + weights:
        copy.start()

    barrier = pltpu.get_barrier_semaphore()

    def seq_peer(step):
        return (lax.rem(seq + step, nseq), chan)

    def z_peer(step):
        return (seq, y * nz + lax.rem(z + step, nz))

    def y_peer(step):
        return (seq, lax.rem(y + step, ny) * nz + z)

    for peer, count in ((z_peer, nz), (y_peer, ny), (seq_peer, nseq)):
        def greet(step, carry, peer=peer):
            pl.semaphore_signal(barrier, inc=1, device_id=peer(step), device_id_type=MESH)
            return carry
        lax.fori_loop(1, count, greet, 0)

    inputs[0].wait()
    slots_y, slots_z = by_distance(ny), by_distance(nz)
    abuf[y, 0] = tok[:half]
    bbuf[z, 0] = tok[half:]
    pl.semaphore_wait(barrier, nz + ny + nseq - 3)

    def first(which, slot):
        slots, source = (slots_z, tok.at[pl.ds(0, half)]) if which == 0 else (slots_y, tok.at[pl.ds(half, half)])
        target = (abuf.at[y] if which == 0 else bbuf.at[z]).at[slot]
        return pltpu.make_async_remote_copy(
            source, target, p1_send.at[which, slot], p1_recv.at[which, slot],
            device_id=(z_peer if which == 0 else y_peer)(len(slots) - slots[slot]), device_id_type=MESH,
        )

    steps = [ny // 2, ny // 2, nz // 2, nz // 2]
    hops = [y_peer(1), y_peer(ny - 1), z_peer(1), z_peer(nz - 1)]
    chunks = [
        [
            lax.rem(place + count - sign * step, count) if step else place
            for step in range(count // 2 + 1)
        ]
        for place, count, sign in ((y, ny, 1), (y, ny, -1), (z, nz, 1), (z, nz, -1))
    ]
    size = [(nz if direction < 2 else ny) // PIECES for direction in range(4)]

    def ring(direction, step, piece, arriving=False):
        buffer = abuf if direction < 2 else bbuf
        chunk = chunks[direction][step if arriving else step - 1]
        block = buffer.at[chunk, pl.ds(piece * size[direction], size[direction])]
        return pltpu.make_async_remote_copy(
            block, block, ring_send.at[direction, step, piece], ring_recv.at[direction, step, piece],
            device_id=hops[direction], device_id_type=MESH,
        )

    def sends(direction, step, piece):
        last = steps[direction]
        return step < last or (step == last and piece % 2 == direction % 2)

    def multiply(direction, chunk, piece):
        count, first_slot = size[direction], piece * size[direction]
        buffer, out = (abuf, pl.ds(0, half)) if direction < 2 else (bbuf, pl.ds(half, half))
        left = jnp.concatenate([buffer[chunk, first_slot + i] for i in range(count)], axis=1)
        right = []
        for i in range(count):
            if direction < 2:
                block = chunk * nz + lax.rem(z + slots_z[first_slot + i], nz)
            else:
                block = lax.rem(y + slots_y[first_slot + i], ny) * nz + chunk
            right.append(w[pl.ds(pl.multiple_of(block * width, width), width)])
        acc[out] += dot(left, jnp.concatenate(right, axis=0))

    def exchange(source, target, send, recv, step):
        to = lax.rem(seq + step, nseq)
        return pltpu.make_async_remote_copy(
            source.at[to], target.at[seq], send.at[step], recv.at[step],
            device_id=(to, chan), device_id_type=MESH,
        )

    others = sorted(range(1, nseq), key=lambda step: abs(step - nseq // 2))
    filters = functools.partial(exchange, fsend, frecv, f_send, f_recv)
    signals = functools.partial(exchange, xsend, xrecv, x_send, x_recv)
    results = functools.partial(exchange, ysend, yrecv, y_send, y_recv)

    for slot in range(1, max(ny, nz)):
        for which, count in ((0, nz), (1, ny)):
            if slot < count:
                first(which, slot).start()
    for copy in inputs[1:]:
        copy.wait()
    fsend[...] = filt[...].T.reshape(nseq, per, rows)
    for step in others:
        filters(step).start()
    frecv[seq] = fsend[seq]
    acc[...] = jnp.zeros_like(acc)

    events = sorted(
        ((step, piece) for step in range(max(steps) + 1) for piece in range(PIECES)),
        key=lambda event: (KEY * event[0] + event[1], event[0]),
    )
    ready = False
    for step, piece in events:
        arrived = []
        for direction in range(4):
            if step == 0:
                if direction % 2 == 0:
                    for slot in range(piece * size[direction], (piece + 1) * size[direction]):
                        if slot:
                            first(direction // 2, slot).wait_recv()
                    arrived.append(direction)
            elif sends(direction, step, piece):
                ring(direction, step, piece, arriving=True).wait_recv()
                arrived.append(direction)
            if (step == 0 or direction in arrived) and sends(direction, step + 1, piece):
                ring(direction, step + 1, piece).start()
        if not ready:
            for copy in weights:
                copy.wait()
            ready = True
        for direction in arrived:
            multiply(direction, chunks[direction][step], piece)

    projection = acc[...].astype(jnp.bfloat16).astype(jnp.float32)
    gate_in, gate_out, values = (projection[:, b * width : (b + 1) * width] for b in range(3))
    grad_dense = gout[...].astype(jnp.float32)
    source = (gate_in * values).T.reshape(nseq, per, rows)
    grad_conv = (grad_dense * gate_out).T.reshape(nseq, per, rows)
    xsend[...] = jnp.concatenate([source, grad_conv], axis=1).astype(jnp.bfloat16)
    for step in others:
        signals(step).start()
    xrecv[seq] = xsend[seq]

    for step in others:
        filters(step).wait_recv()
    for copy in constants:
        copy.wait()
    high, low = split(frecv[...].reshape(nseq * per, rows))
    fspec[...] = (
        dot(jnp.concatenate([high, high], axis=1), fwd[...]) + dot(low, fwd[:rows])
    ).reshape(nseq, per, 2 * rows)

    for step in others:
        signals(step).wait_recv()

    received = xrecv[...].reshape(nseq * 2 * per, rows)
    xspec[...] = dot(jnp.concatenate([received, received], axis=1), fwd[...]).reshape(
        nseq, 2 * per, 2 * rows
    )

    def spectrum(ref, block, first_row):
        return (
            ref[block, first_row : first_row + per, :rows],
            ref[block, first_row : first_row + per, rows:],
        )

    for out in range(nseq):
        re, im = 0.0, 0.0
        for j in range(out + 1):
            f_re, f_im = spectrum(fspec, j, 0)
            s_re, s_im = spectrum(xspec, out - j, 0)
            re = re + (f_re * s_re - f_im * s_im)
            im = im + (f_re * s_im + f_im * s_re)
        prod[out, :per, :rows] = re
        prod[out, :per, rows:] = im
        re, im, re2, im2 = 0.0, 0.0, 0.0, 0.0
        for j in range(nseq - out):
            g_re, g_im = spectrum(xspec, out + j, per)
            f_re, f_im = spectrum(fspec, j, 0)
            s_re, s_im = spectrum(xspec, j, 0)
            re = re + (f_re * g_re + f_im * g_im)
            im = im + (f_re * g_im - f_im * g_re)
            re2 = re2 + (s_re * g_re + s_im * g_im)
            im2 = im2 + (s_re * g_im - s_im * g_re)
        prod[out, per : 2 * per, :rows] = re
        prod[out, per : 2 * per, rows:] = im
        prod[out, 2 * per :, :rows] = re2
        prod[out, 2 * per :, rows:] = im2

    high, low = split(prod[...].reshape(nseq * 3 * per, 2 * rows))
    prod[...] = (dot(high, inv[0]) + dot(low, inv[0]) + dot(high, inv[1])).reshape(
        nseq, 3 * per, 2 * rows
    )
    for block in range(nseq):
        conv = prod[block, :per, :rows]
        grads = prod[block, per:, :rows]
        if block > 0:
            conv = conv + prod[block - 1, :per, rows:]
        if block < nseq - 1:
            grads = grads - prod[block + 1, per:, rows:]
        ysend[block] = jnp.concatenate([conv, grads], axis=0).astype(jnp.bfloat16)
    for step in others:
        results(step).start()
    yrecv[seq] = ysend[seq]
    for step in others:
        results(step).wait_recv()

    back = yrecv[...].astype(jnp.float32)
    conv_out = back[:, :per].reshape(width, rows).T
    grad_source = back[:, per : 2 * per].reshape(width, rows).T
    of_filter = back[:, 2 * per :].reshape(width, rows).T
    gated[...] = (gate_out * conv_out).astype(jnp.bfloat16)
    gproj[0] = (grad_source * values).astype(jnp.bfloat16)
    gproj[1] = (grad_dense * conv_out).astype(jnp.bfloat16)
    gproj[2] = (grad_source * gate_in).astype(jnp.bfloat16)
    gfilt[...] = of_filter

    for which, count in ((0, nz), (1, ny)):
        for slot in range(1, count):
            first(which, slot).wait_send()
    for step, piece in events:
        for direction in range(4):
            if step and sends(direction, step, piece):
                ring(direction, step, piece).wait_send()
    for kind in (filters, signals, results):
        for step in others:
            kind(step).wait_send()


def per_device(tokens, in_weight, long_filter, grad_out):
    rows, width = long_filter.shape
    depth = in_weight.shape[0]
    nseq = lax.axis_size("seq")
    ny, nz = grid_of(lax.axis_size("chan"))
    per = width // nseq
    forward, inverse = tables(rows)
    vmem = pl.BlockSpec(memory_space=pltpu.VMEM)
    hbm = pl.BlockSpec(memory_space=pltpu.HBM)
    bf16, f32 = jnp.bfloat16, jnp.float32
    dma = pltpu.SemaphoreType.DMA
    steps = max(ny, nz) // 2 + 1
    gated_out, grad_proj, grad_filter = pl.pallas_call(
        functools.partial(body, ny, nz, nseq),
        name="gather_project_convolve",
        out_shape=(
            jax.ShapeDtypeStruct((rows, width), bf16),
            jax.ShapeDtypeStruct((3, rows, width), bf16),
            jax.ShapeDtypeStruct((rows, width), f32),
        ),
        in_specs=[hbm] * 6,
        out_specs=(vmem, vmem, vmem),
        scratch_shapes=[
            pltpu.VMEM((rows, width), bf16),
            pltpu.VMEM((rows, width), f32),
            pltpu.VMEM((rows, width), bf16),
            pltpu.VMEM((depth, 3 * width), bf16),
            pltpu.VMEM(forward.shape, bf16),
            pltpu.VMEM(inverse.shape, bf16),
            pltpu.VMEM((ny, nz, rows // 2, width), bf16),
            pltpu.VMEM((nz, ny, rows // 2, width), bf16),
            pltpu.VMEM((rows, 3 * width), f32),
            pltpu.VMEM((nseq, per, rows), f32),
            pltpu.VMEM((nseq, per, rows), f32),
            pltpu.VMEM((nseq, per, 2 * rows), f32),
            pltpu.VMEM((nseq, 2 * per, rows), bf16),
            pltpu.VMEM((nseq, 2 * per, rows), bf16),
            pltpu.VMEM((nseq, 2 * per, 2 * rows), f32),
            pltpu.VMEM((nseq, 3 * per, 2 * rows), f32),
            pltpu.VMEM((nseq, 3 * per, rows), bf16),
            pltpu.VMEM((nseq, 3 * per, rows), bf16),
            dma((8,)),
            dma((2, max(ny, nz))),
            dma((2, max(ny, nz))),
            dma((4, steps, PIECES)),
            dma((4, steps, PIECES)),
            dma((nseq,)),
            dma((nseq,)),
            dma((nseq,)),
            dma((nseq,)),
            dma((nseq,)),
            dma((nseq,)),
        ],
        compiler_params=pltpu.CompilerParams(
            collective_id=0, has_side_effects=True, vmem_limit_bytes=40 * 2**20
        ),
    )(
        *(
            pltpu.with_memory_space_constraint(operand, pltpu.HBM)
            for operand in (
                tokens,
                jnp.transpose(in_weight, (1, 0, 2)),
                long_filter,
                grad_out,
                jnp.asarray(forward),
                jnp.asarray(inverse),
            )
        )
    )
    return gated_out, jnp.transpose(grad_proj, (1, 0, 2)), grad_filter


def solution(mesh):
    in_specs = (P("seq", "chan"), P(None, None, "chan"), P("seq", "chan"), P("seq", "chan"))
    out_specs = (P("seq", "chan"), P("seq", None, "chan"), P("seq", "chan"))
    return jax.shard_map(
        per_device, mesh=mesh, in_specs=in_specs, out_specs=out_specs, check_vma=False
    )
```

```python
import functools
import math

import jax
import jax.numpy as jnp
import ml_dtypes
import numpy as np
from jax import lax
from jax.experimental import pallas as pl
from jax.experimental.pallas import tpu as pltpu
from jax.sharding import PartitionSpec as P

MESH = pl.DeviceIdType.MESH
PIECES = 2
KEY = 3


def by_distance(count):
    return sorted(range(count), key=lambda offset: (min(offset, count - offset), offset))


def grid_of(chans):
    columns = 1
    while columns * columns < chans:
        columns *= 2
    return chans // columns, columns


def split_table(table):
    high = table.astype(ml_dtypes.bfloat16)
    low = (table - high.astype(np.float64)).astype(ml_dtypes.bfloat16)
    return high, low


def tables(rows):
    angle = math.pi * np.outer(np.arange(2 * rows), 2 * np.arange(rows) + 1) / (2 * rows)
    forward = np.concatenate([np.cos(angle), -np.sin(angle)], axis=1)[:rows]
    inverse = np.concatenate([np.cos(angle), -np.sin(angle)], axis=1).T / rows
    return np.concatenate(split_table(forward), axis=0), np.stack(split_table(inverse))


def dot(left, right):
    return jnp.dot(left, right, preferred_element_type=jnp.float32)


def split(value):
    high = value.astype(jnp.bfloat16)
    return high, (value - high.astype(jnp.float32)).astype(jnp.bfloat16)


def body(
    ny, nz, nseq,
    tok_hbm, w_hbm, filt_hbm, gout_hbm, fwd_hbm, inv_hbm,
    gated, gproj, gfilt,
    tok, filt, gout, w, fwd, inv, abuf, bbuf, acc,
    fsend, frecv, fspec, xsend, xrecv, xspec, prod, ysend, yrecv,
    local_sem, p1_send, p1_recv, ring_send, ring_recv, f_send, f_recv, x_send, x_recv, y_send, y_recv,
):
    rows, width = filt.shape
    half = rows // 2
    per = width // nseq
    seq = lax.axis_index("seq")
    chan = lax.axis_index("chan")
    y, z = chan // nz, chan % nz

    weights = [
        pltpu.make_async_copy(w_hbm.at[b], w.at[:, pl.ds(b * width, width)], local_sem.at[b])
        for b in range(3)
    ]
    constants = [
        pltpu.make_async_copy(fwd_hbm, fwd, local_sem.at[3]),
        pltpu.make_async_copy(inv_hbm, inv, local_sem.at[4]),
    ]
    inputs = [
        pltpu.make_async_copy(tok_hbm, tok, local_sem.at[5]),
        pltpu.make_async_copy(filt_hbm, filt, local_sem.at[6]),
        pltpu.make_async_copy(gout_hbm, gout, local_sem.at[7]),
    ]
    for copy in inputs + constants + weights:
        copy.start()

    barrier = pltpu.get_barrier_semaphore()

    def seq_peer(step):
        return (lax.rem(seq + step, nseq), chan)

    def z_peer(step):
        return (seq, y * nz + lax.rem(z + step, nz))

    def y_peer(step):
        return (seq, lax.rem(y + step, ny) * nz + z)

    for peer, count in ((z_peer, nz), (y_peer, ny), (seq_peer, nseq)):
        def greet(step, carry, peer=peer):
            pl.semaphore_signal(barrier, inc=1, device_id=peer(step), device_id_type=MESH)
            return carry
        lax.fori_loop(1, count, greet, 0)

    inputs[0].wait()
    slots_y, slots_z = by_distance(ny), by_distance(nz)
    abuf[y, 0] = tok[:half]
    bbuf[z, 0] = tok[half:]
    pl.semaphore_wait(barrier, nz + ny + nseq - 3)

    def first(which, slot):
        slots, source = (slots_z, tok.at[pl.ds(0, half)]) if which == 0 else (slots_y, tok.at[pl.ds(half, half)])
        target = (abuf.at[y] if which == 0 else bbuf.at[z]).at[slot]
        return pltpu.make_async_remote_copy(
            source, target, p1_send.at[which, slot], p1_recv.at[which, slot],
            device_id=(z_peer if which == 0 else y_peer)(len(slots) - slots[slot]), device_id_type=MESH,
        )

    steps = [ny // 2, ny // 2, nz // 2, nz // 2]
    hops = [y_peer(1), y_peer(ny - 1), z_peer(1), z_peer(nz - 1)]
    chunks = [
        [
            lax.rem(place + count - sign * step, count) if step else place
            for step in range(count // 2 + 1)
        ]
        for place, count, sign in ((y, ny, 1), (y, ny, -1), (z, nz, 1), (z, nz, -1))
    ]
    size = [(nz if direction < 2 else ny) // PIECES for direction in range(4)]

    def ring(direction, step, piece, arriving=False):
        buffer = abuf if direction < 2 else bbuf
        chunk = chunks[direction][step if arriving else step - 1]
        block = buffer.at[chunk, pl.ds(piece * size[direction], size[direction])]
        return pltpu.make_async_remote_copy(
            block, block, ring_send.at[direction, step, piece], ring_recv.at[direction, step, piece],
            device_id=hops[direction], device_id_type=MESH,
        )

    def sends(direction, step, piece):
        last = steps[direction]
        return step < last or (step == last and piece % 2 == direction % 2)

    def multiply(direction, chunk, piece):
        count, first_slot = size[direction], piece * size[direction]
        buffer, out = (abuf, pl.ds(0, half)) if direction < 2 else (bbuf, pl.ds(half, half))
        left = jnp.concatenate([buffer[chunk, first_slot + i] for i in range(count)], axis=1)
        right = []
        for i in range(count):
            if direction < 2:
                block = chunk * nz + lax.rem(z + slots_z[first_slot + i], nz)
            else:
                block = lax.rem(y + slots_y[first_slot + i], ny) * nz + chunk
            right.append(w[pl.ds(pl.multiple_of(block * width, width), width)])
        acc[out] += dot(left, jnp.concatenate(right, axis=0))

    def exchange(source, target, send, recv, step):
        to = lax.rem(seq + step, nseq)
        return pltpu.make_async_remote_copy(
            source.at[to], target.at[seq], send.at[step], recv.at[step],
            device_id=(to, chan), device_id_type=MESH,
        )

    others = sorted(range(1, nseq), key=lambda step: abs(step - nseq // 2))
    filters = functools.partial(exchange, fsend, frecv, f_send, f_recv)
    signals = functools.partial(exchange, xsend, xrecv, x_send, x_recv)
    results = functools.partial(exchange, ysend, yrecv, y_send, y_recv)

    for slot in range(1, max(ny, nz)):
        for which, count in ((0, nz), (1, ny)):
            if slot < count:
                first(which, slot).start()
    for copy in inputs[1:]:
        copy.wait()
    fsend[...] = filt[...].T.reshape(nseq, per, rows)
    for step in others:
        filters(step).start()
    frecv[seq] = fsend[seq]
    acc[...] = jnp.zeros_like(acc)

    events = sorted(
        ((step, piece) for step in range(max(steps) + 1) for piece in range(PIECES)),
        key=lambda event: (KEY * event[0] + event[1], event[0]),
    )
    ready = False
    for step, piece in events:
        arrived = []
        for direction in range(4):
            if step == 0:
                if direction % 2 == 0:
                    for slot in range(piece * size[direction], (piece + 1) * size[direction]):
                        if slot:
                            first(direction // 2, slot).wait_recv()
                    arrived.append(direction)
            elif sends(direction, step, piece):
                ring(direction, step, piece, arriving=True).wait_recv()
                arrived.append(direction)
            if (step == 0 or direction in arrived) and sends(direction, step + 1, piece):
                ring(direction, step + 1, piece).start()
        if not ready:
            for copy in weights:
                copy.wait()
            ready = True
        for direction in arrived:
            multiply(direction, chunks[direction][step], piece)

    projection = acc[...].astype(jnp.bfloat16).astype(jnp.float32)
    gate_in, gate_out, values = (projection[:, b * width : (b + 1) * width] for b in range(3))
    grad_dense = gout[...].astype(jnp.float32)
    source = (gate_in * values).T.reshape(nseq, per, rows)
    grad_conv = (grad_dense * gate_out).T.reshape(nseq, per, rows)
    xsend[...] = jnp.concatenate([source, grad_conv], axis=1).astype(jnp.bfloat16)
    for step in others:
        signals(step).start()
    xrecv[seq] = xsend[seq]

    for step in others:
        filters(step).wait_recv()
    for copy in constants:
        copy.wait()
    high, low = split(frecv[...].reshape(nseq * per, rows))
    fspec[...] = (
        dot(jnp.concatenate([high, high], axis=1), fwd[...]) + dot(low, fwd[:rows])
    ).reshape(nseq, per, 2 * rows)

    for step in others:
        signals(step).wait_recv()

    received = xrecv[...].reshape(nseq * 2 * per, rows)
    xspec[...] = dot(jnp.concatenate([received, received], axis=1), fwd[...]).reshape(
        nseq, 2 * per, 2 * rows
    )

    def spectrum(ref, block, first_row):
        return (
            ref[block, first_row : first_row + per, :rows],
            ref[block, first_row : first_row + per, rows:],
        )

    for out in range(nseq):
        re, im = 0.0, 0.0
        for j in range(out + 1):
            f_re, f_im = spectrum(fspec, j, 0)
            s_re, s_im = spectrum(xspec, out - j, 0)
            re = re + (f_re * s_re - f_im * s_im)
            im = im + (f_re * s_im + f_im * s_re)
        prod[out, :per, :rows] = re
        prod[out, :per, rows:] = im
        re, im, re2, im2 = 0.0, 0.0, 0.0, 0.0
        for j in range(nseq - out):
            g_re, g_im = spectrum(xspec, out + j, per)
            f_re, f_im = spectrum(fspec, j, 0)
            s_re, s_im = spectrum(xspec, j, 0)
            re = re + (f_re * g_re + f_im * g_im)
            im = im + (f_re * g_im - f_im * g_re)
            re2 = re2 + (s_re * g_re + s_im * g_im)
            im2 = im2 + (s_re * g_im - s_im * g_re)
        prod[out, per : 2 * per, :rows] = re
        prod[out, per : 2 * per, rows:] = im
        prod[out, 2 * per :, :rows] = re2
        prod[out, 2 * per :, rows:] = im2

    high, low = split(prod[...].reshape(nseq * 3 * per, 2 * rows))
    prod[...] = (dot(high, inv[0]) + dot(low, inv[0]) + dot(high, inv[1])).reshape(
        nseq, 3 * per, 2 * rows
    )
    for step in others + [0]:
        block = lax.rem(seq + step, nseq)
        before = prod[jnp.maximum(block - 1, 0), :per, rows:]
        after = prod[jnp.minimum(block + 1, nseq - 1), per:, rows:]
        conv = prod[block, :per, :rows] + jnp.where(block > 0, before, 0.0)
        grads = prod[block, per:, :rows] - jnp.where(block < nseq - 1, after, 0.0)
        ysend[block] = jnp.concatenate([conv, grads], axis=0).astype(jnp.bfloat16)
        if step:
            results(step).start()
    yrecv[seq] = ysend[seq]
    for step in others:
        results(step).wait_recv()

    back = yrecv[...].astype(jnp.float32)
    conv_out = back[:, :per].reshape(width, rows).T
    grad_source = back[:, per : 2 * per].reshape(width, rows).T
    of_filter = back[:, 2 * per :].reshape(width, rows).T
    gated[...] = (gate_out * conv_out).astype(jnp.bfloat16)
    gproj[0] = (grad_source * values).astype(jnp.bfloat16)
    gproj[1] = (grad_dense * conv_out).astype(jnp.bfloat16)
    gproj[2] = (grad_source * gate_in).astype(jnp.bfloat16)
    gfilt[...] = of_filter

    for which, count in ((0, nz), (1, ny)):
        for slot in range(1, count):
            first(which, slot).wait_send()
    for step, piece in events:
        for direction in range(4):
            if step and sends(direction, step, piece):
                ring(direction, step, piece).wait_send()
    for kind in (filters, signals, results):
        for step in others:
            kind(step).wait_send()


def per_device(tokens, in_weight, long_filter, grad_out):
    rows, width = long_filter.shape
    depth = in_weight.shape[0]
    nseq = lax.axis_size("seq")
    ny, nz = grid_of(lax.axis_size("chan"))
    per = width // nseq
    forward, inverse = tables(rows)
    vmem = pl.BlockSpec(memory_space=pltpu.VMEM)
    hbm = pl.BlockSpec(memory_space=pltpu.HBM)
    bf16, f32 = jnp.bfloat16, jnp.float32
    dma = pltpu.SemaphoreType.DMA
    steps = max(ny, nz) // 2 + 1
    gated_out, grad_proj, grad_filter = pl.pallas_call(
        functools.partial(body, ny, nz, nseq),
        name="gather_project_convolve",
        out_shape=(
            jax.ShapeDtypeStruct((rows, width), bf16),
            jax.ShapeDtypeStruct((3, rows, width), bf16),
            jax.ShapeDtypeStruct((rows, width), f32),
        ),
        in_specs=[hbm] * 6,
        out_specs=(vmem, vmem, vmem),
        scratch_shapes=[
            pltpu.VMEM((rows, width), bf16),
            pltpu.VMEM((rows, width), f32),
            pltpu.VMEM((rows, width), bf16),
            pltpu.VMEM((depth, 3 * width), bf16),
            pltpu.VMEM(forward.shape, bf16),
            pltpu.VMEM(inverse.shape, bf16),
            pltpu.VMEM((ny, nz, rows // 2, width), bf16),
            pltpu.VMEM((nz, ny, rows // 2, width), bf16),
            pltpu.VMEM((rows, 3 * width), f32),
            pltpu.VMEM((nseq, per, rows), f32),
            pltpu.VMEM((nseq, per, rows), f32),
            pltpu.VMEM((nseq, per, 2 * rows), f32),
            pltpu.VMEM((nseq, 2 * per, rows), bf16),
            pltpu.VMEM((nseq, 2 * per, rows), bf16),
            pltpu.VMEM((nseq, 2 * per, 2 * rows), f32),
            pltpu.VMEM((nseq, 3 * per, 2 * rows), f32),
            pltpu.VMEM((nseq, 3 * per, rows), bf16),
            pltpu.VMEM((nseq, 3 * per, rows), bf16),
            dma((8,)),
            dma((2, max(ny, nz))),
            dma((2, max(ny, nz))),
            dma((4, steps, PIECES)),
            dma((4, steps, PIECES)),
            dma((nseq,)),
            dma((nseq,)),
            dma((nseq,)),
            dma((nseq,)),
            dma((nseq,)),
            dma((nseq,)),
        ],
        compiler_params=pltpu.CompilerParams(
            collective_id=0, has_side_effects=True, vmem_limit_bytes=40 * 2**20
        ),
    )(
        *(
            pltpu.with_memory_space_constraint(operand, pltpu.HBM)
            for operand in (
                tokens,
                jnp.transpose(in_weight, (1, 0, 2)),
                long_filter,
                grad_out,
                jnp.asarray(forward),
                jnp.asarray(inverse),
            )
        )
    )
    return gated_out, jnp.transpose(grad_proj, (1, 0, 2)), grad_filter


def solution(mesh):
    in_specs = (P("seq", "chan"), P(None, None, "chan"), P("seq", "chan"), P("seq", "chan"))
    out_specs = (P("seq", "chan"), P("seq", None, "chan"), P("seq", "chan"))
    return jax.shard_map(
        per_device, mesh=mesh, in_specs=in_specs, out_specs=out_specs, check_vma=False
    )
```
